32 devices in a mesh: basin: 2 (over y), tx: 4 (over z), ty: 2 (over core), ev: 2 (over x).
Axes of the slice: x: 2, y: 2, z: 4, core: 2. Of those that a mesh axis runs over, the one named last changes fastest.
Arguments:
- depth0: float32 [4, 8, 8, 8, 256], P(('basin', 'ev'), None, None, 'tx', 'ty'), parts along dimension 0, may hold values from 0.6 to 1.4
- momentum0: float32 [4, 2, 8, 8, 8, 256], P(('basin', 'ev'), None, None, None, 'tx', 'ty'), parts along dimension 0, may hold values from -2.5 to 2.5
- obs_weight: float32 [4, 8, 8, 8, 256], P(('basin', 'ev'), None, None, 'tx', 'ty'), parts along dimension 0, as said below
- wet_mask: int32 [4, 4, 8, 256], P(('basin', 'ev'), None, 'tx', 'ty'), parts along dimension 0, may hold values 0 or 1
- zone_id: int32 [16, 256], P(('basin', 'tx'), 'ty'), parts along dimension 0, may hold values from 0 to 31
- manning: float32 [64], P('basin'), parts along dimension 0, may hold values from 0.2 to 0.6
Outputs:
- adjoint_state: float32 [4, 3, 8, 8, 8, 256], P(('basin', 'ev'), None, None, None, 'tx', 'ty'), parts along dimension 0
- rough_grad: float32 [64], P('basin'), parts along dimension 0
The draws below stay inside these ranges and needn't reach their ends.
There are 2 independent parts, one for each index of `basin`. The reference program is written for one: setup_inputs(seed, part) draws one part's arguments, and reference() takes and returns one part's arrays. A program takes and returns all parts, laid end to end along the dimension named above; each array names one. Nothing has to cross between parts.
Inputs may be any that keep to these rules, and one draw needn't show every extreme that they name: `wet_mask`: 1 where an element is wet in that section of that event, else 0. `obs_weight`: positive weights.
All inputs are finite; a program needn't handle non-finite values. No bound on the sum of `wet_mask` on one device may be relied on, other than what follows from the above.
Results may differ from the reference program's by a relative error of at most 0.00005.
Values sent between devices are 32-bit elements; how exact they have to be, the bound alone decides.
No kernel may reach another device: no remote copies, remote signals or barrier semaphores. Data moves between devices by JAX's collectives and lax.ppermute only.
A program may use at most 64 MiB of HBM per device.

```python
import math
import jax
import jax.numpy as jnp
import numpy as np
from jax import lax

NP = 8
SECTIONS = 4
ZONES = 32
NEX = 8
NEY = 256
EVENTS = 2


def draw_obs_weight(key, part):
    shape = (EVENTS, NP, NP, NEX, NEY)
    base = jnp.exp(jax.random.uniform(key, shape, jnp.float32, math.log(0.1), math.log(0.3)))
    ramp_event = 1.0 + 2.0 * jnp.arange(EVENTS, dtype=jnp.float32) / max(EVENTS - 1, 1)
    ramp_x = 1.0 + 2.0 * jnp.arange(NEX, dtype=jnp.float32) / max(NEX - 1, 1)
    ramp_y = 1.0 + 2.0 * jnp.arange(NEY, dtype=jnp.float32) / max(NEY - 1, 1)
    return base * ramp_event[:, None, None, None, None] * ramp_x[None, None, None, :, None] * ramp_y[None, None, None, None, :]


def set_ends(array, own_key, least, high):
    extent = array.shape
    spot = [jax.random.randint(jax.random.fold_in(own_key, axis), (), 0, extent[axis]) for axis in range(len(extent))]
    array = array.at[tuple(spot)].set(least)
    longest = extent.index(max(extent))
    spot[longest] = (spot[longest] + 1) % extent[longest]
    return array.at[tuple(spot)].set(high)


def block_scale(key, dims, pieces, least, high):
    def one(dim, parts):
        draws = jax.random.uniform(jax.random.fold_in(jax.random.fold_in(key, 6), dim), (parts,), jnp.float32, least / len(pieces), high / len(pieces))
        return jnp.repeat(jnp.exp(draws), dims[dim] // parts).reshape((-1,) + (1,) * (len(dims) - dim - 1))

    factor_of = one(*pieces[0])
    for cut in pieces[1:]:
        factor_of = factor_of * one(*cut)
    return factor_of


def gaussian(own_key, shape, width, most, shards=(), kind=jnp.bfloat16):
    factor_of = block_scale(own_key, shape, shards, -0.22, 0.18) if shards else 1.0
    values = jax.random.normal(own_key, shape, jnp.float32) * width * factor_of
    return jnp.minimum(jnp.maximum(values, -most), most).astype(kind)


def setup_inputs(seed: int = 0, part: int = 0) -> dict:
    keys = jax.random.split(jax.random.key(seed), 7)
    own_keys = jax.random.split(jax.random.fold_in(keys[6], part), 7)
    depth0 = jnp.clip(0.6 + 0.79999995 * jax.random.uniform(own_keys[0], (EVENTS, NP, NP, NEX, NEY), jnp.float32) ** block_scale(own_keys[0], (EVENTS, NP, NP, NEX, NEY), ((0, 2), (3, 4), (4, 2)), -0.2, 0.2), 0.6, 1.4)
    momentum0 = gaussian(own_keys[1], (EVENTS, 2, NP, NP, NEX, NEY), 0.5, 2.5, ((0, 2), (4, 4), (5, 2)), jnp.float32)
    obs_weight = draw_obs_weight(jax.random.fold_in(jax.random.fold_in(keys[6], part), 71), part)
    wet_mask = set_ends((jax.random.randint(own_keys[3], (EVENTS, SECTIONS, NEX, NEY), 0, 5) < 4).astype(jnp.int32), jax.random.fold_in(own_keys[3], 1), 0, 1)
    zone_id = set_ends(jax.random.randint(own_keys[4], (NEX, NEY), 0, ZONES), jax.random.fold_in(own_keys[4], 1), 0, ZONES - 1).astype(jnp.int32)
    manning = jnp.clip(jnp.exp(jax.random.uniform(own_keys[5], (ZONES,), jnp.float32, math.log(0.2), math.log(0.6))), 0.2, 0.6)
    return {"depth0": depth0, "momentum0": momentum0, "obs_weight": obs_weight, "wet_mask": wet_mask, "zone_id": zone_id, "manning": manning}


GRAVITY = 1.0
PENALTY_SPEED = 4.0
TIME_STEP = 0.0005
SPEED_FLOOR = 0.01

def node_tables():
    points = -np.cos(np.pi * np.arange(NP) / (NP - 1))
    identity = np.eye(NP)
    differ = points[:, None] - points[None, :] + identity
    barycentric = 1.0 / np.prod(differ, axis=1)
    derivative = barycentric[None, :] / barycentric[:, None] / differ * (1.0 - identity)
    derivative = derivative - identity * derivative.sum(axis=1)[:, None]
    order = NP - 1
    if order % 2 == 1:
        end_weight = 1.0 / (order * order)
    else:
        end_weight = 1.0 / (order * order - 1)
    return (derivative, float(1.0 / end_weight))

def fluxes(state, direction):
    depth = state[:, 0]
    flow_x = state[:, 1]
    flow_y = state[:, 2]
    pressure = 0.5 * GRAVITY * depth * depth
    if direction == 0:
        veloc = flow_x / depth
        return jnp.stack([flow_x, flow_x * veloc + pressure, flow_y * veloc], axis=1)
    veloc = flow_y / depth
    return jnp.stack([flow_y, flow_x * veloc, flow_y * veloc + pressure], axis=1)

def face_terms(left_state, right_state, direction, lift_coef):
    flux_left = fluxes(left_state, direction)
    flux_right = fluxes(right_state, direction)
    common = 0.5 * (flux_left + flux_right) - 0.5 * PENALTY_SPEED * (right_state - left_state)
    return (lift_coef * (flux_left - common), lift_coef * (common - flux_right))

def tendency_of(state, neighbours, rough_elem, wet_now, derivative, lift_coef):
    west_nbr, east_nbr, south_nbr, north_nbr = neighbours
    flux_x = fluxes(state, 0)
    flux_y = fluxes(state, 1)
    divergence = jnp.einsum('ai,ecibxy->ecabxy', derivative, flux_x, precision=lax.Precision.HIGHEST)
    divergence = divergence + jnp.einsum('bj,ecajxy->ecabxy', derivative, flux_y, precision=lax.Precision.HIGHEST)
    unused_one, west_term = face_terms(west_nbr, state[:, :, 0], 0, lift_coef)
    east_term, unused_two = face_terms(state[:, :, -1], east_nbr, 0, lift_coef)
    unused_three, south_term = face_terms(south_nbr, state[:, :, :, 0], 1, lift_coef)
    north_term, unused_four = face_terms(state[:, :, :, -1], north_nbr, 1, lift_coef)
    tendency = -divergence
    tendency = tendency.at[:, :, 0].add(west_term)
    tendency = tendency.at[:, :, -1].add(east_term)
    tendency = tendency.at[:, :, :, 0].add(south_term)
    tendency = tendency.at[:, :, :, -1].add(north_term)
    depth = state[:, 0]
    veloc_x = state[:, 1] / depth
    veloc_y = state[:, 2] / depth
    speed_norm = jnp.sqrt(veloc_x * veloc_x + veloc_y * veloc_y + SPEED_FLOOR)
    drag = -GRAVITY * rough_elem * rough_elem * speed_norm / jnp.power(depth, 4.0 / 3.0)
    tendency = tendency.at[:, 1].add(drag * state[:, 1])
    tendency = tendency.at[:, 2].add(drag * state[:, 2])
    return wet_now[:, None, None, None] * tendency

def neighbors(state):
    own_west = state[:, :, 0]
    own_east = state[:, :, -1]
    own_south = state[:, :, :, 0]
    own_north = state[:, :, :, -1]
    west_nbr = jnp.concatenate([own_west[:, :, :, :1], own_east[:, :, :, :-1]], axis=3)
    east_nbr = jnp.concatenate([own_west[:, :, :, 1:], own_east[:, :, :, -1:]], axis=3)
    south_nbr = jnp.concatenate([own_south[:, :, :, :, :1], own_north[:, :, :, :, :-1]], axis=4)
    north_nbr = jnp.concatenate([own_south[:, :, :, :, 1:], own_north[:, :, :, :, -1:]], axis=4)
    return (west_nbr, east_nbr, south_nbr, north_nbr)

def reference(depth0, momentum0, obs_weight, wet_mask, zone_id, manning):
    table, lift_coef = node_tables()
    derivative = jnp.asarray(table, jnp.float32)

    def one_event(inputs):
        depth_event, momentum_event, weight_event, wet_event = inputs
        start = jnp.concatenate([depth_event[None, None], momentum_event[None]], axis=1)

        def forward(start_state, rough):
            rough_elem = rough[zone_id]

            def section_rhs(state, section_index):
                wet_now = wet_event[section_index][None].astype(jnp.float32)
                return tendency_of(state, neighbors(state), rough_elem, wet_now, derivative, lift_coef)
            slope_one = section_rhs(start_state, 0)
            slope_two = section_rhs(start_state + 0.5 * TIME_STEP * slope_one, 1)
            slope_three = section_rhs(start_state + 0.5 * TIME_STEP * slope_two, 2)
            slope_four = section_rhs(start_state + TIME_STEP * slope_three, 3)
            return start_state + TIME_STEP / 6.0 * (slope_one + 2.0 * slope_two + 2.0 * slope_three + slope_four)
        final, pullback = jax.vjp(forward, start, manning)
        adjoint_final = jnp.stack([jnp.zeros_like(final[:, 0]), weight_event[None] * final[:, 1], weight_event[None] * final[:, 2]], axis=1)
        adjoint_start, rough_cot = pullback(adjoint_final)
        return (adjoint_start[0], rough_cot)
    adjoint_state, rough_cots = lax.map(one_event, (depth0, momentum0, obs_weight, wet_mask))
    scale = ZONES / (TIME_STEP * EVENTS * NEX * NEY * NP * NP)
    return (adjoint_state, lax.optimization_barrier(jnp.sum(rough_cots, axis=0)) * scale)
```

```python
import functools

import jax
import jax.numpy as jnp
import numpy as np
from jax import lax
from jax.experimental import pallas as pl
from jax.experimental.pallas import tpu as pltpu
from jax.sharding import PartitionSpec as P

NP = 8
NODES = NP * NP
LANES = 128
HALO = 8
PENALTY_SPEED = 4.0
TIME_STEP = 0.0005
SPEED_FLOOR = 0.01
COEFS = (0.5 * TIME_STEP, 0.5 * TIME_STEP, TIME_STEP)
WEIGHTS = (TIME_STEP / 6.0, TIME_STEP / 3.0, TIME_STEP / 3.0, TIME_STEP / 6.0)
F32 = jnp.float32
BF16 = jnp.bfloat16


def node_tables():
    points = -np.cos(np.pi * np.arange(NP) / (NP - 1))
    identity = np.eye(NP)
    differ = points[:, None] - points[None, :] + identity
    barycentric = 1.0 / np.prod(differ, axis=1)
    derivative = barycentric[None, :] / barycentric[:, None] / differ * (1.0 - identity)
    derivative = derivative - identity * derivative.sum(axis=1)[:, None]
    order = NP - 1
    end_weight = 1.0 / (order * order)
    return (derivative, float(1.0 / end_weight))


def split_table(table):
    table = np.asarray(table, np.float32)
    high = table.astype(BF16)
    low = (table - high.astype(np.float32)).astype(BF16)
    return np.concatenate([high, high, low], axis=1)


def split_dot(table, data):
    high = data.astype(BF16)
    low = (data - high.astype(F32)).astype(BF16)
    return jnp.dot(table, jnp.concatenate([high, low, high], axis=0), preferred_element_type=F32)


class Plan:
    def __init__(self, parts, cols, rows):
        self.parts = parts
        self.cols = cols
        self.width = rows // parts
        assert rows == LANES and parts * self.width == rows and self.width >= HALO
        self.window = self.width + 2 * HALO
        full, rest = divmod(self.window, self.width)
        self.segments = []
        tile = 0
        for column in range(cols):
            for piece in range(full):
                self.segments.append((tile, column, piece * self.width, self.width, 0))
                tile += 1
        if rest:
            per_tile = self.width // rest
            assert per_tile * rest == self.width
            for column in range(cols):
                self.segments.append(
                    (tile + column // per_tile, column, full * self.width, rest, column % per_tile * rest)
                )
            tile += -(-cols // per_tile)
        self.tiles = tile

    def find(self, column, row):
        for seg in self.segments:
            if seg[1] == column and seg[2] <= row < seg[2] + seg[3]:
                return seg
        return None

    def moves(self, side):
        table = [[] for _ in range(self.tiles)]
        for tile, column, first, count, offset in self.segments:
            if side in ("west", "east"):
                step = -1 if side == "west" else 1
                other = column + step
                wrap = 0
                if other < 0 or other >= self.cols:
                    wrap = step
                    other -= step * self.cols
                src = self.find(other, first)
                table[tile].append((src[0], src[4] - offset + wrap * self.width, offset, offset + count))
            else:
                step = -1 if side == "south" else 1
                table[tile].append((tile, step, offset, offset + count))
                edge = first - 1 if side == "south" else first + count
                src = self.find(column, edge)
                if src is not None:
                    at = offset if side == "south" else offset + count - 1
                    src_at = src[4] + edge - src[2]
                    table[tile].append((src[0], src_at - at, at, at + 1))
        merged = []
        for entries in table:
            kept = []
            for entry in entries:
                if kept and kept[-1][:2] == entry[:2] and kept[-1][3] == entry[2]:
                    kept[-1] = entry[:2] + (kept[-1][2], entry[3])
                else:
                    kept.append(entry)
            merged.append(kept)
        return merged


def roll(x, shift):
    shift = shift % LANES
    return x if shift == 0 else pltpu.roll(x, shift, 1)


def lane_iota(rows=8):
    return lax.broadcasted_iota(jnp.int32, (rows, LANES), 1)


def shifted(tiles, moves, width, offset_of):
    out = []
    for entries in moves:
        value = None
        for src, distance, first, end in entries:
            moved = roll(tiles[src], -distance)
            if value is None:
                value = moved
            else:
                value = jnp.where((offset_of >= first) & (offset_of < end), moved, value)
        out.append(value)
    return out


def exchange_out(pieces, put, me, parts, width):
    slot = lane_iota() // width
    for group in range(-(-len(pieces) // parts)):
        turned = []
        for j in range(parts):
            n = group * parts + j
            turned.append(roll(pieces[n](), width * j) if n < len(pieces) else None)
        for m in range(parts):
            dest = me ^ m
            turn = (slot - dest) & (parts - 1)
            value = turned[0]
            for j in range(1, parts):
                if turned[j] is not None:
                    value = jnp.where(turn == j, turned[j], value)
            put(m, group, value)


def exchange_in(get, count, me, parts, width):
    slot = lane_iota() // width
    for group in range(-(-count // parts)):
        turned = []
        for m in range(parts):
            source = me ^ m
            value = get(m, group)
            if m:
                value = pltpu.roll(value, ((source - me) & (parts - 1)) * width, 1)
            turned.append((source, value))
        for j in range(parts):
            n = group * parts + j
            if n < count:
                from_slot = (slot - j) & (parts - 1)
                value = turned[0][1]
                for source, other in turned[1:]:
                    value = jnp.where(from_slot == source, other, value)
                yield n, roll(value, -width * j)


def source_vreg(refs, array, i, column, cols):
    depth, momentum, weight, wet, zone = refs
    if array == 4:
        parts = [wet[0, :, column, :].astype(F32), zone[column : column + 1, :].astype(F32)]
        return jnp.concatenate(parts + [jnp.zeros((3, LANES), F32)], axis=0)
    ref = (depth, momentum, momentum, weight)[array]
    index = i + (NP if array == 2 else 0)
    return ref[index, pl.ds(column, NP, stride=cols), :]


SOURCES = [(array, i) for array in range(4) for i in range(NP)] + [(4, 0)]
PER_VREG = LANES // HALO


def halo_kernel(cols, depth, momentum, weight, wet, zone, out):
    refs = (depth, momentum, weight, wet, zone)
    first = lax.axis_index("ty") == 0
    base = jnp.where(first, HALO, 0)
    slot = lane_iota() // HALO
    count = len(SOURCES) * cols
    for group in range(-(-count // PER_VREG)):
        value = jnp.zeros((8, LANES), F32)
        for k in range(PER_VREG):
            n = group * PER_VREG + k
            if n < count:
                (array, i), column = SOURCES[n // cols], n % cols
                moved = pltpu.roll(
                    source_vreg(refs, array, i, column, cols), (base + HALO * k) & (LANES - 1), 1
                )
                value = jnp.where(slot == k, moved, value)
        out[group] = value


def pack_kernel(plan, depth, momentum, weight, wet, zone, halo, *outs):
    refs = (depth, momentum, weight, wet, zone)
    me = lax.axis_index("tx")
    lane = lane_iota()
    offset_of = lane & (plan.width - 1)
    cols, width, parts = plan.cols, plan.width, plan.parts

    def window_piece(array, i, number, tile):
        value = None
        for seg_tile, column, first, count, offset in plan.segments:
            if seg_tile != tile:
                continue
            own = roll(source_vreg(refs, array, i, column, cols), offset - (first - HALO))
            n = number * cols + column
            remote = halo[n // PER_VREG]
            at = HALO * (n % PER_VREG)
            if first < HALO:
                start = offset
                own = jnp.where(
                    (lane >= start) & (lane < start + HALO - first), roll(remote, start - at - first), own
                )
            if first + count > width + HALO:
                begin = max(first, width + HALO)
                start = (parts - 1) * width + offset + begin - first
                length = first + count - begin
                own = jnp.where(
                    (lane >= start) & (lane < start + length),
                    roll(remote, start - at - (begin - width - HALO)),
                    own,
                )
            if value is None:
                value = own
            else:
                value = jnp.where((offset_of >= offset) & (offset_of < offset + count), own, value)
        return value

    pieces = [
        functools.partial(window_piece, array, i, number, tile)
        for number, (array, i) in enumerate(SOURCES)
        for tile in range(plan.tiles)
    ]

    def put(m, group, value):
        outs[m][group] = value

    exchange_out(pieces, put, me, parts, width)


def step_kernel(plan, lift, *refs):
    parts, width, cols, tiles = plan.parts, plan.width, plan.cols, plan.tiles
    messages = refs[:parts]
    man_ref, fwd_table, adj_table, top_table = refs[parts : parts + 4]
    outs = refs[parts + 4 : 2 * parts + 4]
    rough_out = refs[2 * parts + 4]
    state, weight, wet, ground, flux, slope, speed, rub, final, later, masked, pull = refs[2 * parts + 5 :]
    me = lax.axis_index("tx")
    ty = lax.axis_index("ty")
    ty_last = lax.axis_size("ty") - 1
    lane = lane_iota()
    offset_of = lane & (width - 1)
    slot = lane // width
    zones = man_ref.shape[1]

    aux = [None] * tiles
    for n, value in exchange_in(
        lambda m, group: messages[m][group], len(SOURCES) * tiles, me, parts, width
    ):
        (array, i), tile = SOURCES[n // tiles], n % tiles
        if array < 3:
            state[0, tile, array, i] = value
        elif array == 3:
            weight[tile, i] = value
        else:
            aux[tile] = value
    zone_iota = lax.broadcasted_iota(jnp.int32, (zones, LANES), 0).astype(F32)
    hot = []
    rough = []
    row_of = []
    column_of = []
    man = jnp.broadcast_to(man_ref[...], (8, zones))
    for tile in range(tiles):
        for s in range(4):
            wet[s, tile] = jnp.broadcast_to(aux[tile][s : s + 1], (8, LANES))
        hot.append((jnp.broadcast_to(aux[tile][4:5], (zones, LANES)) == zone_iota).astype(F32))
        rough.append(jnp.dot(man, hot[tile], precision=lax.Precision.HIGHEST, preferred_element_type=F32))
        ground[tile] = rough[tile] * rough[tile]
        row = None
        for seg_tile, column, first, count, offset in plan.segments:
            if seg_tile == tile:
                here_row, here_col = offset_of - offset + first, slot * cols + column
                if row is None:
                    row, col = here_row, here_col
                else:
                    inside = (offset_of >= offset) & (offset_of < offset + count)
                    row, col = jnp.where(inside, here_row, row), jnp.where(inside, here_col, col)
        row_of.append(row)
        column_of.append(col)
    block_row = me * width - HALO
    inner = {
        "west": [col > 0 for col in column_of],
        "east": [col < parts * cols - 1 for col in column_of],
        "south": [(row + block_row != 0) | (ty != 0) for row in row_of],
        "north": [(row + block_row != parts * width - 1) | (ty != ty_last) for row in row_of],
    }
    moves = {side: plan.moves(side) for side in inner}

    def neighbour(values, side):
        return shifted(values, moves[side], width, offset_of)

    def kept(side, tile, value):
        return jnp.where(inner[side][tile], value, 0.0)

    def low(ref, index):
        return [ref[(tile,) + index + (pl.ds(0, NP, stride=NP), slice(None))] for tile in range(tiles)]

    def high(ref, index):
        return [
            ref[(tile,) + index + (pl.ds(NP - 1, NP, stride=NP), slice(None))] for tile in range(tiles)
        ]

    half = 0.5 * lift
    drive = PENALTY_SPEED
    for s in range(4):
        comps = (0, 1, 2) if s < 3 else (1, 2)
        for tile in range(tiles):
            for i in range(NP):
                h, m, n = (state[s, tile, c, i] for c in range(3))
                inverse = 1.0 / h
                u, v = m * inverse, n * inverse
                pressure = 0.5 * h * h
                across = n * u
                square = u * u + v * v + SPEED_FLOOR
                root = lax.rsqrt(square)
                drag = -(square * root) * jnp.exp((-4.0 / 3.0) * jnp.log(h))
                speed[s, tile, 0, i] = inverse
                speed[s, tile, 1, i] = u
                speed[s, tile, 2, i] = v
                rub[s, tile, 0, i] = drag
                rub[s, tile, 1, i] = drag * (root * root)
                rows = pl.ds(i * NP, NP)
                flux[tile, 0, rows] = m
                flux[tile, 1, rows] = n
                flux[tile, 2, rows] = m * u + pressure
                flux[tile, 3, rows] = across
                flux[tile, 4, rows] = n * v + pressure
        for c in comps:
            pair = (0, 2, 3)[c]
            data = jnp.concatenate(
                [
                    jnp.concatenate([flux[tile, pair], flux[tile, pair + 1]], axis=0)
                    for tile in range(tiles)
                ],
                axis=1,
            )
            out = split_dot(fwd_table[...], data)
            for tile in range(tiles):
                slope[tile, c] = out[:, tile * LANES : (tile + 1) * LANES]
        for c in comps:
            index = (0, 2, 3)[c]
            west_f = [flux[t, index, pl.ds(0, NP)] for t in range(tiles)]
            east_f = [flux[t, index, pl.ds(NODES - NP, NP)] for t in range(tiles)]
            west_q = [drive * state[s, t, c, 0] for t in range(tiles)]
            east_q = [drive * state[s, t, c, NP - 1] for t in range(tiles)]
            from_west = neighbour([f + q for f, q in zip(east_f, east_q)], "west")
            from_east = neighbour([f - q for f, q in zip(west_f, west_q)], "east")
            for t in range(tiles):
                slope[t, c, pl.ds(0, NP)] += kept("west", t, half * (from_west[t] - (west_f[t] + west_q[t])))
                slope[t, c, pl.ds(NODES - NP, NP)] += kept(
                    "east", t, half * ((east_f[t] - east_q[t]) - from_east[t])
                )
            index = (1, 3, 4)[c]
            south_f, north_f = low(flux, (index,)), high(flux, (index,))
            south_q = [
                drive * jnp.concatenate([state[s, t, c, i, 0:1] for i in range(NP)], axis=0) for t in range(tiles)
            ]
            north_q = [
                drive * jnp.concatenate([state[s, t, c, i, NP - 1 : NP] for i in range(NP)], axis=0)
                for t in range(tiles)
            ]
            from_south = neighbour([f + q for f, q in zip(north_f, north_q)], "south")
            from_north = neighbour([f - q for f, q in zip(south_f, south_q)], "north")
            for t in range(tiles):
                rows = pl.ds(0, NP, stride=NP)
                slope[t, c, rows] += kept("south", t, half * (from_south[t] - (south_f[t] + south_q[t])))
                rows = pl.ds(NP - 1, NP, stride=NP)
                slope[t, c, rows] += kept("north", t, half * ((north_f[t] - north_q[t]) - from_north[t]))
        for tile in range(tiles):
            now = wet[s, tile]
            for i in range(NP):
                rows = pl.ds(i * NP, NP)
                drag = ground[tile] * rub[s, tile, 0, i]
                for c in comps:
                    value = slope[tile, c, rows]
                    if c:
                        value = value + drag * state[s, tile, c, i]
                    value = now * value
                    if s < 3:
                        state[s + 1, tile, c, i] = state[0, tile, c, i] + COEFS[s] * value
                    if c:
                        total = state[0, tile, c, i] if s == 0 else final[tile, c - 1, i]
                        total = total + WEIGHTS[s] * value
                        final[tile, c - 1, i] = weight[tile, i] * total if s == 3 else total

    gathered = [jnp.zeros((8, LANES), F32) for _ in range(tiles)]
    for s in (3, 2, 1, 0):
        comps = (0, 1, 2) if s < 3 else (1, 2)
        for tile in range(tiles):
            now = wet[s, tile]
            for i in range(NP):
                rows = pl.ds(i * NP, NP)
                for c in comps:
                    value = WEIGHTS[s] * final[tile, c - 1, i] if c else None
                    if s < 3:
                        carried = COEFS[s] * later[tile, c, rows]
                        value = carried if value is None else value + carried
                    masked[tile, c, rows] = now * value
        both = jnp.concatenate(
            [jnp.concatenate([masked[t, 1], masked[t, 2]], axis=0) for t in range(tiles)], axis=1
        )
        out = split_dot(adj_table[...], both)
        for t in range(tiles):
            for k in range(3):
                pull[t, 2 + k] = out[k * NODES : (k + 1) * NODES, t * LANES : (t + 1) * LANES]
        if s < 3:
            data = jnp.concatenate([masked[t, 0] for t in range(tiles)], axis=1)
            out = split_dot(top_table[...], data)
            for t in range(tiles):
                for k in range(2):
                    pull[t, k] = out[k * NODES : (k + 1) * NODES, t * LANES : (t + 1) * LANES]
        direct = []
        for c in comps:
            first, last = pl.ds(0, NP), pl.ds(NODES - NP, NP)
            x_index, y_index = (0, 2, 3)[c], (1, 3, 4)[c]
            for name, other, mine, theirs, index, sign in (
                ("west", "east", first, last, x_index, -1.0),
                ("east", "west", last, first, x_index, 1.0),
                ("south", "north", pl.ds(0, NP, stride=NP), pl.ds(NP - 1, NP, stride=NP), y_index, -1.0),
                ("north", "south", pl.ds(NP - 1, NP, stride=NP), pl.ds(0, NP, stride=NP), y_index, 1.0),
            ):
                own = [masked[t, c, mine] for t in range(tiles)]
                beside = neighbour([masked[t, c, theirs] for t in range(tiles)], name)
                for t in range(tiles):
                    pull[t, index, mine] += kept(name, t, (sign * half) * (own[t] + beside[t]))
                    direct.append((t, c, mine, kept(name, t, (half * drive) * (beside[t] - own[t]))))
        for tile in range(tiles):
            for i in range(NP):
                rows = pl.ds(i * NP, NP)
                h, m, n = (state[s, tile, c, i] for c in range(3))
                inverse, u, v = (speed[s, tile, k, i] for k in range(3))
                cot_m, cot_n = masked[tile, 1, rows], masked[tile, 2, rows]
                along = cot_m * m + cot_n * n
                rubbed = rub[s, tile, 0, i] * along
                gathered[tile] = gathered[tile] + rubbed
                drag = ground[tile] * rub[s, tile, 0, i]
                extra = ground[tile] * rub[s, tile, 1, i] * along * inverse
                x_m, mixed, y_n = (pull[tile, 2 + k, rows] for k in range(3))
                uu, vv = u * u, v * v
                later_h = (
                    (h - uu) * x_m
                    + (h - vv) * y_n
                    - u * v * mixed
                    - extra * (uu + vv)
                    - (4.0 / 3.0) * (ground[tile] * rubbed) * inverse
                )
                later_m = 2.0 * u * x_m + v * mixed + drag * cot_m + extra * u
                later_n = 2.0 * v * y_n + u * mixed + drag * cot_n + extra * v
                if s < 3:
                    later_m = later_m + pull[tile, 0, rows]
                    later_n = later_n + pull[tile, 1, rows]
                later[tile, 0, rows] = later_h
                later[tile, 1, rows] = later_m
                later[tile, 2, rows] = later_n
        for t, c, rows, value in direct:
            later[t, c, rows] += value
        for tile in range(tiles):
            for i in range(NP):
                rows = pl.ds(i * NP, NP)
                for c in range(3):
                    value = later[tile, c, rows]
                    if s < 3:
                        value = value + slope[tile, c, rows]
                    elif c:
                        value = value + final[tile, c - 1, i]
                    slope[tile, c, rows] = value

    part = jnp.zeros((8, zones), F32)
    for tile in range(tiles):
        own_rows = (row_of[tile] >= HALO) & (row_of[tile] < HALO + width)
        sums = jnp.broadcast_to(jnp.sum(gathered[tile], axis=0, keepdims=True), (8, LANES))
        sums = jnp.where(own_rows, 2.0 * rough[tile] * sums, 0.0)
        part = part + lax.dot_general(
            sums,
            hot[tile],
            (((1,), (1,)), ((), ())),
            precision=lax.Precision.HIGHEST,
            preferred_element_type=F32,
        )
    rough_out[...] = jnp.concatenate([part, jnp.zeros((8, LANES - zones), F32)], axis=1)

    def own_piece(c, i, column):
        value = None
        for tile, seg_col, first, count, offset in plan.segments:
            begin, end = max(first, HALO), min(first + count, HALO + width)
            if seg_col != column or begin >= end:
                continue
            moved = roll(slope[tile, c, pl.ds(i * NP, NP)], (begin - HALO) - (offset + begin - first))
            if value is None:
                value = moved
            else:
                value = jnp.where((offset_of >= begin - HALO) & (offset_of < end - HALO), moved, value)
        return value

    pieces = [
        functools.partial(own_piece, c, i, column) for c in range(3) for i in range(NP) for column in range(cols)
    ]

    def put(m, group, value):
        outs[m][group] = value

    exchange_out(pieces, put, me, parts, width)


def finish_kernel(plan, *refs):
    parts, width, cols = plan.parts, plan.width, plan.cols
    messages = refs[:parts]
    (out,) = refs[parts:]
    me = lax.axis_index("tx")
    count = 3 * NP * cols
    for n, value in exchange_in(lambda m, group: messages[m][group], count, me, parts, width):
        plane, column = n // cols, n % cols
        out[plane, pl.ds(column, NP, stride=cols), :] = value


def call(kernel, outs, scratch=(), flops=1000000):
    return pl.pallas_call(
        kernel,
        out_shape=outs,
        scratch_shapes=scratch,
        compiler_params=pltpu.CompilerParams(vmem_limit_bytes=16 << 20),
        cost_estimate=pl.CostEstimate(flops=flops, bytes_accessed=1000000, transcendentals=0),
    )


def xor_swap(value, axis, bits):
    count = lax.axis_size(axis)
    return lax.ppermute(value, axis, [(i, i ^ bits) for i in range(count)])


def local(depth0, momentum0, obs_weight, wet_mask, zone_id, manning):
    table, lift = node_tables()
    cols, rows = depth0.shape[3], depth0.shape[4]
    parts = lax.axis_size("tx")
    plan = Plan(parts, cols, rows)
    zones = manning.shape[0]
    depth = depth0.reshape(NP, NP * cols, rows)
    momentum = momentum0.reshape(2 * NP, NP * cols, rows)
    weight = obs_weight.reshape(NP, NP * cols, rows)
    fields = (depth, momentum, weight, wet_mask, zone_id)

    def out(*shape):
        return jax.ShapeDtypeStruct(shape, F32)

    groups = -(-len(SOURCES) * cols // PER_VREG)
    halo = call(functools.partial(halo_kernel, cols), out(groups, 8, LANES))(*fields)
    if lax.axis_size("ty") > 1:
        assert lax.axis_size("ty") == 2
        halo = xor_swap(halo, "ty", 1)
    count = -(-len(SOURCES) * plan.tiles // parts)
    sent = call(functools.partial(pack_kernel, plan), [out(count, 8, LANES)] * parts)(*fields, halo)
    received = [sent[0]] + [xor_swap(sent[m], "tx", m) for m in range(1, parts)]

    along_i, along_j = np.kron(table, np.eye(NP)), np.kron(np.eye(NP), table)
    nothing = np.zeros_like(along_i)
    fwd_table = split_table(-np.concatenate([along_i, along_j], axis=1))
    adj_table = split_table(
        -np.block([[along_i.T, nothing], [along_j.T, along_i.T], [nothing, along_j.T]])
    )
    top_table = split_table(-np.concatenate([along_i.T, along_j.T], axis=0))
    back = -(-3 * NP * cols // parts)
    t = plan.tiles
    scratch = [
        pltpu.VMEM((4, t, 3, NP, NP, LANES), F32),
        pltpu.VMEM((t, NP, NP, LANES), F32),
        pltpu.VMEM((4, t, NP, LANES), F32),
        pltpu.VMEM((t, NP, LANES), F32),
        pltpu.VMEM((t, 5, NODES, LANES), F32),
        pltpu.VMEM((t, 3, NODES, LANES), F32),
        pltpu.VMEM((4, t, 3, NP, NP, LANES), F32),
        pltpu.VMEM((4, t, 2, NP, NP, LANES), F32),
        pltpu.VMEM((t, 2, NP, NP, LANES), F32),
        pltpu.VMEM((t, 3, NODES, LANES), F32),
        pltpu.VMEM((t, 3, NODES, LANES), F32),
        pltpu.VMEM((t, 5, NODES, LANES), F32),
    ]
    results = call(
        functools.partial(step_kernel, plan, lift),
        [out(back, 8, LANES)] * parts + [out(8, LANES)],
        scratch,
    )(
        *received,
        manning.reshape(1, zones),
        jnp.asarray(fwd_table),
        jnp.asarray(adj_table),
        jnp.asarray(top_table),
    )
    answers, rough = results[:parts], results[parts]
    for axis in ("ev", "ty", "tx"):
        bit = 1
        while bit < lax.axis_size(axis):
            rough = rough + xor_swap(rough, axis, bit)
            bit *= 2
    answers = [answers[0]] + [xor_swap(answers[m], "tx", m) for m in range(1, parts)]
    adjoint = call(functools.partial(finish_kernel, plan), out(3 * NP, NP * cols, rows))(*answers)
    events_all = depth0.shape[0] * lax.axis_size("ev")
    scale = zones / (TIME_STEP * events_all * cols * parts * rows * lax.axis_size("ty") * NODES)
    return (adjoint.reshape(1, 3, NP, NP, cols, rows), rough[0, :zones] * scale)


def solution(mesh):
    in_specs = (
        P(("basin", "ev"), None, None, "tx", "ty"),
        P(("basin", "ev"), None, None, None, "tx", "ty"),
        P(("basin", "ev"), None, None, "tx", "ty"),
        P(("basin", "ev"), None, "tx", "ty"),
        P(("basin", "tx"), "ty"),
        P("basin"),
    )
    out_specs = (P(("basin", "ev"), None, None, None, "tx", "ty"), P("basin"))
    return jax.shard_map(local, mesh=mesh, in_specs=in_specs, out_specs=out_specs, check_vma=False)
```

```python
import functools

import jax
import jax.numpy as jnp
import numpy as np
from jax import lax
from jax.experimental import pallas as pl
from jax.experimental.pallas import tpu as pltpu
from jax.sharding import PartitionSpec as P


NP = 8
NODES = NP * NP
LANES = 128
HALO = 8
PENALTY_SPEED = 4.0
TIME_STEP = 0.0005
SPEED_FLOOR = 0.01
COEFS = (0.5 * TIME_STEP, 0.5 * TIME_STEP, TIME_STEP)
WEIGHTS = (TIME_STEP / 6.0, TIME_STEP / 3.0, TIME_STEP / 3.0, TIME_STEP / 6.0)
F32 = jnp.float32
BF16 = jnp.bfloat16


def node_tables():
    points = -np.cos(np.pi * np.arange(NP) / (NP - 1))
    identity = np.eye(NP)
    differ = points[:, None] - points[None, :] + identity
    barycentric = 1.0 / np.prod(differ, axis=1)
    derivative = barycentric[None, :] / barycentric[:, None] / differ * (1.0 - identity)
    derivative = derivative - identity * derivative.sum(axis=1)[:, None]
    order = NP - 1
    end_weight = 1.0 / (order * order)
    return (derivative, float(1.0 / end_weight))


def split_table(main, ends):
    main = np.asarray(main, np.float32)
    high = main.astype(BF16)
    low = (main - high.astype(np.float32)).astype(BF16)
    ends = ends.astype(BF16)
    return np.concatenate([high, high, low, ends, ends], axis=1)


def split_data(main, ends):
    halves = []
    for blocks in (main, ends):
        data = jnp.concatenate(blocks, axis=0)
        high = data.astype(BF16)
        halves.append((high, (data - high.astype(F32)).astype(BF16)))
    (high, low), (end_high, end_low) = halves
    return jnp.concatenate([high, low, high, end_high, end_low], axis=0)


class Plan:
    def __init__(self, parts, cols, rows):
        self.parts = parts
        self.cols = cols
        self.width = rows // parts
        assert rows == LANES and parts * self.width == rows and self.width >= HALO
        self.window = self.width + 2 * HALO
        full, rest = divmod(self.window, self.width)
        self.segments = []
        tile = 0
        for column in range(cols):
            for piece in range(full):
                self.segments.append((tile, column, piece * self.width, self.width, 0))
                tile += 1
        if rest:
            per_tile = self.width // rest
            assert per_tile * rest == self.width
            for column in range(cols):
                self.segments.append(
                    (tile + column // per_tile, column, full * self.width, rest, column % per_tile * rest)
                )
            tile += -(-cols // per_tile)
        self.tiles = tile

    def find(self, column, row):
        for seg in self.segments:
            if seg[1] == column and seg[2] <= row < seg[2] + seg[3]:
                return seg
        return None

    def moves(self, side):
        table = [[] for _ in range(self.tiles)]
        for tile, column, first, count, offset in self.segments:
            if side in ("west", "east"):
                step = -1 if side == "west" else 1
                other = column + step
                wrap = 0
                if other < 0 or other >= self.cols:
                    wrap = step
                    other -= step * self.cols
                src = self.find(other, first)
                table[tile].append((src[0], src[4] - offset + wrap * self.width, offset, offset + count))
            else:
                step = -1 if side == "south" else 1
                table[tile].append((tile, step, offset, offset + count))
                edge = first - 1 if side == "south" else first + count
                src = self.find(column, edge)
                if src is not None:
                    at = offset if side == "south" else offset + count - 1
                    src_at = src[4] + edge - src[2]
                    table[tile].append((src[0], src_at - at, at, at + 1))
        merged = []
        for entries in table:
            kept = []
            for entry in entries:
                if kept and kept[-1][:2] == entry[:2] and kept[-1][3] == entry[2]:
                    kept[-1] = entry[:2] + (kept[-1][2], entry[3])
                else:
                    kept.append(entry)
            merged.append(kept)
        return merged


def roll(x, shift):
    shift = shift % LANES
    return x if shift == 0 else pltpu.roll(x, shift, 1)


def lane_iota(rows=8):
    return lax.broadcasted_iota(jnp.int32, (rows, LANES), 1)


def shifted(tiles, moves, offset_of):
    out = []
    for entries in moves:
        value = None
        for src, distance, first, end in entries:
            moved = roll(tiles[src], -distance)
            if value is None:
                value = moved
            else:
                value = jnp.where((offset_of >= first) & (offset_of < end), moved, value)
        out.append(value)
    return out


def exchange_out(pieces, put, me, parts, width):
    slot = lane_iota() // width
    for group in range(-(-len(pieces) // parts)):
        turned = []
        for j in range(parts):
            n = group * parts + j
            turned.append(roll(pieces[n](), width * j) if n < len(pieces) else None)
        for m in range(parts):
            dest = me ^ m
            turn = (slot - dest) & (parts - 1)
            value = turned[0]
            for j in range(1, parts):
                if turned[j] is not None:
                    value = jnp.where(turn == j, turned[j], value)
            put(m, group, value)


def exchange_in(get, count, me, parts, width):
    slot = lane_iota() // width
    for group in range(-(-count // parts)):
        turned = []
        for m in range(parts):
            source = me ^ m
            value = get(m, group)
            if m:
                value = pltpu.roll(value, ((source - me) & (parts - 1)) * width, 1)
            turned.append((source, value))
        for j in range(parts):
            n = group * parts + j
            if n < count:
                from_slot = (slot - j) & (parts - 1)
                value = turned[0][1]
                for source, other in turned[1:]:
                    value = jnp.where(from_slot == source, other, value)
                yield n, roll(value, -width * j)


def source_vreg(refs, array, i, column, cols):
    depth, momentum, weight, wet, zone = refs
    if array == 4:
        parts = [wet[0, :, column, :].astype(F32), zone[column : column + 1, :].astype(F32)]
        return jnp.concatenate(parts + [jnp.zeros((3, LANES), F32)], axis=0)
    ref = (depth, momentum, momentum, weight)[array]
    index = i + (NP if array == 2 else 0)
    return ref[index, pl.ds(column, NP, stride=cols), :]


SOURCES = [(array, i) for array in range(4) for i in range(NP)] + [(4, 0)]
PER_VREG = LANES // HALO


def chunks(count):
    size = NP // 2
    return [pl.ds(k, size) for k in range(0, count, size)] if count % size == 0 else [pl.ds(0, count)]


def halo_kernel(cols, *refs):
    sources, (copies, out, sems) = refs[:6], (refs[6:12], refs[12], refs[13])
    moves = []
    for src, dst in zip(sources, copies):
        for rows in chunks(src.shape[0]):
            moves.append(pltpu.make_async_copy(src.at[rows], dst.at[rows], sems.at[len(moves)]))
    for move in moves:
        move.start()
    for move in moves:
        move.wait()
    first = lax.axis_index("ty") == 0
    base = jnp.where(first, HALO, 0)
    slot = lane_iota() // HALO
    count = len(SOURCES) * cols
    for group in range(-(-count // PER_VREG)):
        value = jnp.zeros((8, LANES), F32)
        for k in range(PER_VREG):
            n = group * PER_VREG + k
            if n < count:
                (array, i), column = SOURCES[n // cols], n % cols
                moved = pltpu.roll(
                    source_vreg(copies[:5], array, i, column, cols), (base + HALO * k) & (LANES - 1), 1
                )
                value = jnp.where(slot == k, moved, value)
        out[group] = value


def turn_kernel(plan, depth, momentum, weight, wet, zone, out):
    refs = (depth, momentum, weight, wet, zone)
    offset_of = lane_iota() & (plan.width - 1)
    for number, (array, i) in enumerate(SOURCES):
        columns = [source_vreg(refs, array, i, column, plan.cols) for column in range(plan.cols)]
        for tile in range(plan.tiles):
            piece = number * plan.tiles + tile
            turn = plan.width * (piece % plan.parts)
            value = None
            for seg_tile, column, first, count, offset in plan.segments:
                if seg_tile == tile:
                    own = roll(columns[column], turn + offset - (first - HALO))
                    if value is None:
                        value = own
                    else:
                        at = (offset_of >= offset) & (offset_of < offset + count)
                        value = jnp.where(at, own, value)
            out[piece] = value


def pack_kernel(plan, turned, halo, *outs):
    me = lax.axis_index("tx")
    lane = lane_iota()
    cols, width, parts = plan.cols, plan.width, plan.parts
    slot = lane // width
    pieces = turned.shape[0]

    def within(start, length):
        return ((lane - start) & (LANES - 1)) < length

    def piece_with_halo(piece):
        number, tile = piece // plan.tiles, piece % plan.tiles
        turn = width * (piece % parts)
        value = turned[piece]
        for seg_tile, column, first, count, offset in plan.segments:
            if seg_tile != tile:
                continue
            n = number * cols + column
            remote, at = halo[n // PER_VREG], HALO * (n % PER_VREG)
            if first < HALO:
                start = (turn + offset) % LANES
                value = jnp.where(within(start, HALO - first), roll(remote, start - at - first), value)
            if first + count > width + HALO:
                begin = max(first, width + HALO)
                start = (turn + (parts - 1) * width + offset + begin - first) % LANES
                length = first + count - begin
                shift = start - at - (begin - width - HALO)
                value = jnp.where(within(start, length), roll(remote, shift), value)
        return value

    for group in range(-(-pieces // parts)):
        values = [
            piece_with_halo(group * parts + j) if group * parts + j < pieces else None for j in range(parts)
        ]
        for m in range(parts):
            turn = (slot - (me ^ m)) & (parts - 1)
            value = values[0]
            for j in range(1, parts):
                if values[j] is not None:
                    value = jnp.where(turn == j, values[j], value)
            outs[m][group] = value


class Geometry:
    def __init__(self, plan):
        self.plan = plan
        width, cols, parts = plan.width, plan.cols, plan.parts
        me, ty, ty_last = lax.axis_index("tx"), lax.axis_index("ty"), lax.axis_size("ty") - 1
        lane = lane_iota()
        self.offset_of = lane & (width - 1)
        slot = lane // width
        self.row_of, self.column_of = [], []
        for tile in range(plan.tiles):
            row = None
            for seg_tile, column, first, count, offset in plan.segments:
                if seg_tile == tile:
                    here_row, here_col = self.offset_of - offset + first, slot * cols + column
                    if row is None:
                        row, col = here_row, here_col
                    else:
                        inside = (self.offset_of >= offset) & (self.offset_of < offset + count)
                        row, col = jnp.where(inside, here_row, row), jnp.where(inside, here_col, col)
            self.row_of.append(row)
            self.column_of.append(col)
        block_row = me * width - HALO
        self.inner = {
            "west": [col > 0 for col in self.column_of],
            "east": [col < parts * cols - 1 for col in self.column_of],
            "south": [(row + block_row != 0) | (ty != 0) for row in self.row_of],
            "north": [(row + block_row != parts * width - 1) | (ty != ty_last) for row in self.row_of],
        }
        self.moves = {side: plan.moves(side) for side in self.inner}

    def neighbour(self, values, side):
        return shifted(values, self.moves[side], self.offset_of)

    def kept(self, side, tile, value):
        return jnp.where(self.inner[side][tile], value, 0.0)


SIDES = (
    ("west", "east", pl.ds(0, NP), -1.0),
    ("east", "west", pl.ds(NODES - NP, NP), 1.0),
    ("south", "north", pl.ds(0, NP, stride=NP), -1.0),
    ("north", "south", pl.ds(NP - 1, NP, stride=NP), 1.0),
)


def cut(value, i):
    return value[i * NP : (i + 1) * NP]


def section_adjoint(s, geometry, lift, adj_table, state, wet, speed, rub, final, later, total, gathered):
    half, drive = 0.5 * lift, PENALTY_SPEED
    neighbour, kept = geometry.neighbour, geometry.kept
    every = range(geometry.plan.tiles)
    comps = (0, 1, 2) if s < 3 else (1, 2)
    given = [WEIGHTS[s] * wet[s, t] for t in every]
    passed = [COEFS[s] * wet[s, t] if s < 3 else None for t in every]

    def masked(t, c, rows):
        value = given[t] * final[t, c - 1, rows] if c else None
        if s < 3:
            carried = passed[t] * later[s + 1, t, c, rows]
            value = carried if value is None else value + carried
        return value

    trace = {(name, c, t): masked(t, c, rows) for name, _, rows, _ in SIDES for c in comps for t in every}
    pulls, direct = {}, {}
    for name, other, _, sign in SIDES:
        for c in comps:
            beside = neighbour([trace[other, c, t] for t in every], name)
            for t in every:
                own = trace[name, c, t]
                pulls[name, c, t] = kept(name, t, (sign * half) * (own + beside[t]))
                direct[name, c, t] = kept(name, t, (half * drive) * (beside[t] - own))
    for t in every:
        cots = [[masked(t, c, pl.ds(i * NP, NP)) for i in range(NP)] for c in range(3)]
        ends = lambda c: [table[name, c, t] for table in (pulls, direct) for name in ("south", "north")]
        data = jnp.concatenate([split_data(cots[c], ends(c)) for c in comps], axis=1)
        out = jnp.dot(adj_table[...], data, preferred_element_type=F32)
        columns = {c: out[:, at * LANES : (at + 1) * LANES] for at, c in enumerate(comps)}
        for i in range(NP):
            rows = pl.ds(i * NP, NP)
            pull_x, pull_y, adds = (
                {c: cut(columns[c], k * NP + i) for c in comps} for k in range(3)
            )
            x_m, mixed, y_n = pull_x[1], pull_y[1] + pull_x[2], pull_y[2]
            to_m, to_n = adds[1], adds[2]
            if s < 3:
                to_m, to_n, to_h = to_m + pull_x[0], to_n + pull_y[0], adds[0]
            for at, name in ((0, "west"), (NP - 1, "east")):
                if i == at:
                    x_m = x_m + pulls[name, 1, t]
                    mixed = mixed + pulls[name, 2, t]
                    to_m = to_m + direct[name, 1, t]
                    to_n = to_n + direct[name, 2, t]
                    if s < 3:
                        to_m = to_m + pulls[name, 0, t]
                        to_h = to_h + direct[name, 0, t]
            h, u, v = state[s, t, 0, rows], speed[s, t, 0, rows], speed[s, t, 1, rows]
            cot_m, cot_n = cots[1][i], cots[2][i]
            drag, over = rub[s, t, 0, rows], rub[s, t, 1, rows]
            along = cot_m * u + cot_n * v
            fall = drag * along
            extra = over * along
            if gathered is not None:
                gathered[t] = gathered[t] + fall * h
            ux, vy = u * x_m, v * y_n
            first = ux + v * mixed + extra * u
            second = vy + extra * v
            later_h = h * (x_m + y_n) - u * first - v * second - (4.0 / 3.0) * fall
            if s < 3:
                later_h = later_h + to_h
            later_m = to_m + ux + first + drag * cot_m
            later_n = to_n + (vy + u * mixed) + second + drag * cot_n
            for c, value in enumerate((later_h, later_m, later_n)):
                if s == 0:
                    value = value + (later[1, t, c, rows] + later[2, t, c, rows] + later[3, t, c, rows])
                    if c:
                        value = value + final[t, c - 1, rows]
                    total[t, c, rows] = value
                else:
                    later[s, t, c, rows] = value


def step_kernel(plan, lift, *refs):
    parts, width, tiles = plan.parts, plan.width, plan.tiles
    messages = refs[:parts]
    man_ref, fwd_table, adj_table = refs[parts : parts + 3]
    rough_out, state, wet, speed, rub, final, later = refs[parts + 3 : parts + 10]
    weight, drop = refs[parts + 10 :]
    me = lax.axis_index("tx")
    zones = man_ref.shape[1]
    half, drive = 0.5 * lift, PENALTY_SPEED
    every = range(tiles)

    aux = [None] * tiles
    for n, value in exchange_in(
        lambda m, group: messages[m][group], len(SOURCES) * tiles, me, parts, width
    ):
        (array, i), tile = SOURCES[n // tiles], n % tiles
        if array < 3:
            state[0, tile, array, pl.ds(i * NP, NP)] = value
        elif array == 3:
            weight[tile, pl.ds(i * NP, NP)] = value
        else:
            aux[tile] = value
    geometry = Geometry(plan)
    neighbour, kept, row_of = geometry.neighbour, geometry.kept, geometry.row_of
    zone_iota = lax.broadcasted_iota(jnp.int32, (zones, LANES), 0).astype(F32)
    hot = []
    rough = []
    man = jnp.broadcast_to(man_ref[...], (8, zones))
    for tile in range(tiles):
        for s in range(4):
            wet[s, tile] = jnp.broadcast_to(aux[tile][s : s + 1], (8, LANES))
        hot.append((jnp.broadcast_to(aux[tile][4:5], (zones, LANES)) == zone_iota).astype(F32))
        rough.append(jnp.dot(man, hot[tile], precision=lax.Precision.HIGHEST, preferred_element_type=F32))
        drop[tile] = -(rough[tile] * rough[tile])

    for s in range(4):
        comps = (0, 1, 2) if s < 3 else (1, 2)
        for t in every:
            for i in range(NP):
                rows = pl.ds(i * NP, NP)
                h, m, n = (state[s, t, c, rows] for c in range(3))
                inverse = 1.0 / h
                u, v = m * inverse, n * inverse
                square = u * u + v * v + SPEED_FLOOR
                over = drop[t] * (lax.rsqrt(square) * jnp.exp((-4.0 / 3.0) * jnp.log(h)))
                speed[s, t, 0, rows] = u
                speed[s, t, 1, rows] = v
                rub[s, t, 0, rows] = over * square
                rub[s, t, 1, rows] = over
        hands, keeps = {}, {}
        for name, _, rows, sign in SIDES:
            for t in every:
                h, m, n = (state[s, t, c, rows] for c in range(3))
                pressure = 0.5 * h * h
                if name in ("west", "east"):
                    u = speed[s, t, 0, rows]
                    parts_of = (m, m * u + pressure, n * u)
                else:
                    v = speed[s, t, 1, rows]
                    parts_of = (n, m * v, n * v + pressure)
                for c in comps:
                    f, q = parts_of[c], (sign * drive) * (h, m, n)[c]
                    hands[name, c, t] = f + q
                    keeps[name, c, t] = f - q
        gains = {}
        for name, other, _, sign in SIDES:
            for c in comps:
                beside = neighbour([hands[other, c, t] for t in every], name)
                for t in every:
                    gains[name, c, t] = kept(name, t, (sign * half) * (keeps[name, c, t] - beside[t]))
        for t in every:
            fluxes = [[] for _ in range(5)]
            for i in range(NP):
                rows = pl.ds(i * NP, NP)
                h, m, n = (state[s, t, c, rows] for c in range(3))
                u, v = speed[s, t, 0, rows], speed[s, t, 1, rows]
                pressure = 0.5 * h * h
                for k, value in enumerate((m, n, m * u + pressure, n * u, n * v + pressure)):
                    fluxes[k].append(value)
            columns = []
            for c in comps:
                first, second = ((0, 1), (2, 3), (3, 4))[c]
                columns.append(
                    split_data(fluxes[first] + fluxes[second], [gains["south", c, t], gains["north", c, t]])
                )
            out = jnp.dot(
                fwd_table[...], jnp.concatenate(columns, axis=1), preferred_element_type=F32
            )
            now = (COEFS[s] if s < 3 else WEIGHTS[3]) * wet[s, t]
            for at, c in enumerate(comps):
                for i in range(NP):
                    rows = pl.ds(i * NP, NP)
                    value = cut(out[:, at * LANES : (at + 1) * LANES], i)
                    if i == 0:
                        value = value + gains["west", c, t]
                    if i == NP - 1:
                        value = value + gains["east", c, t]
                    if c:
                        value = value + rub[s, t, 0, rows] * state[s, t, c, rows]
                    start = state[0, t, c, rows]
                    if s < 3:
                        state[s + 1, t, c, rows] = start + now * value
                    else:
                        middle = state[1, t, c, rows] + 2.0 * state[2, t, c, rows] + state[3, t, c, rows]
                        total = ((1.0 / 3.0) * middle - (1.0 / 3.0) * start) + now * value
                        final[t, c - 1, rows] = weight[t, rows] * total

    gathered = [jnp.zeros((8, LANES), F32) for _ in every]
    for s in (3, 2, 1):
        section_adjoint(
            s, geometry, lift, adj_table, state, wet, speed, rub, final, later, None, gathered
        )
    gather_first(state, wet, speed, rub, final, later, gathered)

    part = jnp.zeros((8, zones), F32)
    for tile in range(tiles):
        own_rows = (row_of[tile] >= HALO) & (row_of[tile] < HALO + width)
        sums = jnp.broadcast_to(jnp.sum(gathered[tile], axis=0, keepdims=True), (8, LANES))
        sums = jnp.where(own_rows, 2.0 * sums / rough[tile], 0.0)
        part = part + lax.dot_general(
            sums,
            hot[tile],
            (((1,), (1,)), ((), ())),
            precision=lax.Precision.HIGHEST,
            preferred_element_type=F32,
        )
    rough_out[...] = jnp.concatenate([part, jnp.zeros((8, LANES - zones), F32)], axis=1)


def gather_first(state, wet, speed, rub, final, later, gathered):
    for t in range(len(gathered)):
        given, passed = WEIGHTS[0] * wet[0, t], COEFS[0] * wet[0, t]
        for i in range(NP):
            rows = pl.ds(i * NP, NP)
            cot_m, cot_n = (given * final[t, c - 1, rows] + passed * later[1, t, c, rows] for c in (1, 2))
            along = cot_m * speed[0, t, 0, rows] + cot_n * speed[0, t, 1, rows]
            gathered[t] = gathered[t] + rub[0, t, 0, rows] * along * state[0, t, 0, rows]


def answer_kernel(plan, lift, adj_table, state, wet, speed, rub, final, later, *refs):
    parts, width, cols = plan.parts, plan.width, plan.cols
    outs, total = refs[:parts], refs[parts]
    me = lax.axis_index("tx")
    geometry = Geometry(plan)
    offset_of = geometry.offset_of
    section_adjoint(0, geometry, lift, adj_table, state, wet, speed, rub, final, later, total, None)

    def own_piece(c, i, column):
        value = None
        for tile, seg_col, first, count, offset in plan.segments:
            begin, end = max(first, HALO), min(first + count, HALO + width)
            if seg_col != column or begin >= end:
                continue
            moved = roll(total[tile, c, pl.ds(i * NP, NP)], (begin - HALO) - (offset + begin - first))
            if value is None:
                value = moved
            else:
                value = jnp.where((offset_of >= begin - HALO) & (offset_of < end - HALO), moved, value)
        return value

    pieces = [
        functools.partial(own_piece, c, i, column) for c in range(3) for i in range(NP) for column in range(cols)
    ]

    def put(m, group, value):
        outs[m][group] = value

    exchange_out(pieces, put, me, parts, width)


def stamp_kernel(parts, *refs):
    mine, other, outs = refs[parts], refs[parts + 1], refs[parts + 2 :]
    total = mine[...] + other[...]
    for out in outs:
        out[out.shape[0] - 1] = total


def finish_kernel(plan, *refs):
    parts, width, cols = plan.parts, plan.width, plan.cols
    messages = refs[:parts]
    (out,) = refs[parts:]
    me = lax.axis_index("tx")
    count = 3 * NP * cols
    for n, value in exchange_in(lambda m, group: messages[m][group], count, me, parts, width):
        plane, column = n // cols, n % cols
        out[plane, pl.ds(column, NP, stride=cols), :] = value


def call(kernel, outs, scratch=(), flops=1000000):
    return pl.pallas_call(
        kernel,
        out_shape=outs,
        scratch_shapes=scratch,
        compiler_params=pltpu.CompilerParams(vmem_limit_bytes=16 << 20),
        cost_estimate=pl.CostEstimate(flops=flops, bytes_accessed=1000000, transcendentals=0),
    )


def xor_swap(value, axis, bits):
    count = lax.axis_size(axis)
    return lax.ppermute(value, axis, [(i, i ^ bits) for i in range(count)])


def sum_over(value, axis):
    count, bit = lax.axis_size(axis), 1
    while bit < count:
        if 4 * bit <= count:
            one, two, three = (xor_swap(value, axis, k * bit) for k in (1, 2, 3))
            value = (value + one) + (two + three)
            bit *= 4
        else:
            value = value + xor_swap(value, axis, bit)
            bit *= 2
    return value


def local(depth0, momentum0, obs_weight, wet_mask, zone_id, manning):
    table, lift = node_tables()
    cols, rows = depth0.shape[3], depth0.shape[4]
    parts = lax.axis_size("tx")
    plan = Plan(parts, cols, rows)
    zones = manning.shape[0]
    depth = depth0.reshape(NP, NP * cols, rows)
    momentum = momentum0.reshape(2 * NP, NP * cols, rows)
    weight = obs_weight.reshape(NP, NP * cols, rows)
    fields = (depth, momentum, weight, wet_mask, zone_id)

    def out(*shape):
        return jax.ShapeDtypeStruct(shape, F32)

    groups = -(-len(SOURCES) * cols // PER_VREG)
    inputs = fields + (manning.reshape(1, zones),)
    inputs = tuple(pltpu.with_memory_space_constraint(x, pltpu.HBM) for x in inputs)
    results = pl.pallas_call(
        functools.partial(halo_kernel, cols),
        out_shape=[jax.ShapeDtypeStruct(x.shape, x.dtype) for x in inputs] + [out(groups, 8, LANES)],
        in_specs=[pl.BlockSpec(memory_space=pltpu.HBM)] * 6,
        scratch_shapes=[pltpu.SemaphoreType.DMA((sum(len(chunks(x.shape[0])) for x in inputs),))],
        compiler_params=pltpu.CompilerParams(vmem_limit_bytes=16 << 20),
        cost_estimate=pl.CostEstimate(flops=1000000, bytes_accessed=1000000, transcendentals=0),
    )(*inputs)
    fields, man, halo = results[:5], results[5], results[6]
    if lax.axis_size("ty") > 1:
        assert lax.axis_size("ty") == 2
        halo = xor_swap(halo, "ty", 1)
    pieces = len(SOURCES) * plan.tiles
    count = -(-pieces // parts)
    turned = call(functools.partial(turn_kernel, plan), out(pieces, 8, LANES))(*fields)
    sent = call(functools.partial(pack_kernel, plan), [out(count, 8, LANES)] * parts)(turned, halo)
    received = [sent[0]] + [xor_swap(sent[m], "tx", m) for m in range(1, parts)]

    along_i, along_j = np.kron(table, np.eye(NP)), np.kron(np.eye(NP), table)
    ends = np.concatenate([np.kron(np.eye(NP), np.eye(NP)[:, k : k + 1]) for k in (0, NP - 1)], axis=1)
    none = np.zeros_like(ends)
    fwd_table = split_table(np.concatenate([-along_i, -along_j], axis=1), ends)
    adj_table = split_table(
        np.concatenate([-along_i.T, -along_j.T, np.zeros_like(along_i)], axis=0),
        np.block([[none, none], [ends, none], [none, ends]]),
    )
    back = -(-3 * NP * cols // parts)
    t = plan.tiles
    shapes = [
        (4, t, 3, NODES, LANES),
        (4, t, NP, LANES),
        (4, t, 2, NODES, LANES),
        (4, t, 2, NODES, LANES),
        (t, 2, NODES, LANES),
        (4, t, 3, NODES, LANES),
    ]
    tables = jnp.asarray(fwd_table), jnp.asarray(adj_table)
    rough, *kept = call(
        functools.partial(step_kernel, plan, lift),
        [out(8, LANES)] + [out(*shape) for shape in shapes],
        [pltpu.VMEM((t, NODES, LANES), F32), pltpu.VMEM((t, NP, LANES), F32)],
    )(*received, man, *tables)
    answers = call(
        functools.partial(answer_kernel, plan, lift),
        [out(back + 1, 8, LANES)] * parts,
        [pltpu.VMEM((t, 3, NODES, LANES), F32)],
    )(tables[1], *kept)
    other = jnp.zeros_like(rough)
    if lax.axis_size("ev") == 2:
        other = xor_swap(rough, "ev", 1)
    elif lax.axis_size("ev") > 1:
        rough = sum_over(rough, "ev")
    space = pl.BlockSpec(memory_space=pltpu.VMEM)
    answers = pl.pallas_call(
        functools.partial(stamp_kernel, parts),
        out_shape=[out(back + 1, 8, LANES)] * parts,
        in_specs=[pl.BlockSpec(memory_space=pl.ANY)] * parts + [space] * 2,
        out_specs=[space] * parts,
        input_output_aliases={m: m for m in range(parts)},
        compiler_params=pltpu.CompilerParams(vmem_limit_bytes=16 << 20),
        cost_estimate=pl.CostEstimate(flops=1000, bytes_accessed=1000, transcendentals=0),
    )(*answers, rough, other)
    answers = [answers[0]] + [xor_swap(answers[m], "tx", m) for m in range(1, parts)]
    sums = [answer[back] for answer in answers]
    while len(sums) > 1:
        sums = [one + two for one, two in zip(sums[::2], sums[1::2])]
    rough = sum_over(sums[0], "ty")
    adjoint = call(functools.partial(finish_kernel, plan), out(3 * NP, NP * cols, rows))(*answers)
    events_all = depth0.shape[0] * lax.axis_size("ev")
    scale = zones / (TIME_STEP * events_all * cols * parts * rows * lax.axis_size("ty") * NODES)
    return (adjoint.reshape(1, 3, NP, NP, cols, rows), rough[0, :zones] * scale)


def solution(mesh):
    in_specs = (
        P(("basin", "ev"), None, None, "tx", "ty"),
        P(("basin", "ev"), None, None, None, "tx", "ty"),
        P(("basin", "ev"), None, None, "tx", "ty"),
        P(("basin", "ev"), None, "tx", "ty"),
        P(("basin", "tx"), "ty"),
        P("basin"),
    )
    out_specs = (P(("basin", "ev"), None, None, None, "tx", "ty"), P("basin"))
    return jax.shard_map(local, mesh=mesh, in_specs=in_specs, out_specs=out_specs, check_vma=False)
```

```python
import functools

import jax
import jax.numpy as jnp
import numpy as np
from jax import lax
from jax.experimental import pallas as pl
from jax.experimental.pallas import tpu as pltpu
from jax.sharding import PartitionSpec as P


NP = 8
NODES = NP * NP
LANES = 128
HALO = 8
PENALTY_SPEED = 4.0
TIME_STEP = 0.0005
SPEED_FLOOR = 0.01
COEFS = (0.5 * TIME_STEP, 0.5 * TIME_STEP, TIME_STEP)
WEIGHTS = (TIME_STEP / 6.0, TIME_STEP / 3.0, TIME_STEP / 3.0, TIME_STEP / 6.0)
F32 = jnp.float32
BF16 = jnp.bfloat16


def node_tables():
    points = -np.cos(np.pi * np.arange(NP) / (NP - 1))
    identity = np.eye(NP)
    differ = points[:, None] - points[None, :] + identity
    barycentric = 1.0 / np.prod(differ, axis=1)
    derivative = barycentric[None, :] / barycentric[:, None] / differ * (1.0 - identity)
    derivative = derivative - identity * derivative.sum(axis=1)[:, None]
    order = NP - 1
    end_weight = 1.0 / (order * order)
    return (derivative, float(1.0 / end_weight))


def split_table(main, ends):
    main = np.asarray(main, np.float32)
    high = main.astype(BF16)
    low = (main - high.astype(np.float32)).astype(BF16)
    ends = ends.astype(BF16)
    return np.concatenate([high, high, low, ends, ends], axis=1)


def split_data(main, ends):
    halves = []
    for blocks in (main, ends):
        data = jnp.concatenate(blocks, axis=0)
        high = data.astype(BF16)
        halves.append((high, (data - high.astype(F32)).astype(BF16)))
    (high, low), (end_high, end_low) = halves
    return jnp.concatenate([high, low, high, end_high, end_low], axis=0)


class Plan:
    def __init__(self, parts, cols, rows):
        self.parts = parts
        self.cols = cols
        self.width = rows // parts
        assert rows == LANES and parts * self.width == rows and self.width >= HALO
        self.window = self.width + 2 * HALO
        full, rest = divmod(self.window, self.width)
        self.segments = []
        tile = 0
        for column in range(cols):
            for piece in range(full):
                self.segments.append((tile, column, piece * self.width, self.width, 0))
                tile += 1
        if rest:
            per_tile = self.width // rest
            assert per_tile * rest == self.width
            for column in range(cols):
                self.segments.append(
                    (tile + column // per_tile, column, full * self.width, rest, column % per_tile * rest)
                )
            tile += -(-cols // per_tile)
        self.tiles = tile

    def find(self, column, row):
        for seg in self.segments:
            if seg[1] == column and seg[2] <= row < seg[2] + seg[3]:
                return seg
        return None

    def moves(self, side):
        table = [[] for _ in range(self.tiles)]
        for tile, column, first, count, offset in self.segments:
            if side in ("west", "east"):
                step = -1 if side == "west" else 1
                other = column + step
                wrap = 0
                if other < 0 or other >= self.cols:
                    wrap = step
                    other -= step * self.cols
                src = self.find(other, first)
                table[tile].append((src[0], src[4] - offset + wrap * self.width, offset, offset + count))
            else:
                step = -1 if side == "south" else 1
                table[tile].append((tile, step, offset, offset + count))
                edge = first - 1 if side == "south" else first + count
                src = self.find(column, edge)
                if src is not None:
                    at = offset if side == "south" else offset + count - 1
                    src_at = src[4] + edge - src[2]
                    table[tile].append((src[0], src_at - at, at, at + 1))
        merged = []
        for entries in table:
            kept = []
            for entry in entries:
                if kept and kept[-1][:2] == entry[:2] and kept[-1][3] == entry[2]:
                    kept[-1] = entry[:2] + (kept[-1][2], entry[3])
                else:
                    kept.append(entry)
            merged.append(kept)
        return merged


def roll(x, shift):
    shift = shift % LANES
    return x if shift == 0 else pltpu.roll(x, shift, 1)


def lane_iota(rows=8):
    return lax.broadcasted_iota(jnp.int32, (rows, LANES), 1)


def shifted(tiles, moves, offset_of):
    out = []
    for entries in moves:
        value = None
        for src, distance, first, end in entries:
            moved = roll(tiles[src], -distance)
            if value is None:
                value = moved
            else:
                value = jnp.where((offset_of >= first) & (offset_of < end), moved, value)
        out.append(value)
    return out


def exchange_out(pieces, put, me, parts, width):
    slot = lane_iota() // width
    for group in range(-(-len(pieces) // parts)):
        turned = []
        for j in range(parts):
            n = group * parts + j
            turned.append(roll(pieces[n](), width * j) if n < len(pieces) else None)
        for m in range(parts):
            dest = me ^ m
            turn = (slot - dest) & (parts - 1)
            value = turned[0]
            for j in range(1, parts):
                if turned[j] is not None:
                    value = jnp.where(turn == j, turned[j], value)
            put(m, group, value)


def exchange_in(get, count, me, parts, width):
    slot = lane_iota() // width
    for group in range(-(-count // parts)):
        turned = []
        for m in range(parts):
            source = me ^ m
            value = get(m, group)
            if m:
                value = pltpu.roll(value, ((source - me) & (parts - 1)) * width, 1)
            turned.append((source, value))
        for j in range(parts):
            n = group * parts + j
            if n < count:
                from_slot = (slot - j) & (parts - 1)
                value = turned[0][1]
                for source, other in turned[1:]:
                    value = jnp.where(from_slot == source, other, value)
                yield n, roll(value, -width * j)


def source_vreg(refs, array, i, column, cols):
    depth, momentum, weight, wet, zone = refs
    if array == 4:
        parts = [wet[0, :, column, :].astype(F32), zone[column : column + 1, :].astype(F32)]
        return jnp.concatenate(parts + [jnp.zeros((3, LANES), F32)], axis=0)
    ref = (depth, momentum, momentum, weight)[array]
    index = i + (NP if array == 2 else 0)
    return ref[index, pl.ds(column, NP, stride=cols), :]


EARLY = [(array, i) for array in range(3) for i in range(NP)] + [(4, 0)]
LATE = [(3, i) for i in range(NP)]
SOURCES = EARLY + LATE
PER_VREG = LANES // HALO


def chunks(count):
    size = NP // 2
    whole = count % size != 0 or count > 2 * NP
    return [pl.ds(0, count)] if whole else [pl.ds(k, size) for k in range(0, count, size)]


def halo_kernel(cols, *refs):
    count = (len(refs) - 2) // 2
    sources, copies, out, sems = refs[:count], refs[count:-2], refs[-2], refs[-1]
    moves = []
    for src, dst in zip(sources, copies):
        for rows in chunks(src.shape[0]):
            moves.append(pltpu.make_async_copy(src.at[rows], dst.at[rows], sems.at[len(moves)]))
    needed = sum(len(chunks(src.shape[0])) for src in sources[:5])
    for move in moves:
        move.start()
    for move in moves[:needed]:
        move.wait()
    first = lax.axis_index("ty") == 0
    base = jnp.where(first, HALO, 0)
    slot = lane_iota() // HALO
    count = len(SOURCES) * cols
    for group in range(-(-count // PER_VREG)):
        value = jnp.zeros((8, LANES), F32)
        for k in range(PER_VREG):
            n = group * PER_VREG + k
            if n < count:
                (array, i), column = SOURCES[n // cols], n % cols
                moved = pltpu.roll(
                    source_vreg(copies[:5], array, i, column, cols), (base + HALO * k) & (LANES - 1), 1
                )
                value = jnp.where(slot == k, moved, value)
        out[group] = value
    for move in moves[needed:]:
        move.wait()


def turn_kernel(plan, depth, momentum, weight, wet, zone, *outs):
    refs = (depth, momentum, weight, wet, zone)
    offset_of = lane_iota() & (plan.width - 1)
    for sources, out in zip((EARLY, LATE), outs):
        for number, (array, i) in enumerate(sources):
            columns = [source_vreg(refs, array, i, column, plan.cols) for column in range(plan.cols)]
            for tile in range(plan.tiles):
                piece = number * plan.tiles + tile
                turn = plan.width * (piece % plan.parts)
                value = None
                for seg_tile, column, first, count, offset in plan.segments:
                    if seg_tile == tile:
                        own = roll(columns[column], turn + offset - (first - HALO))
                        if value is None:
                            value = own
                        else:
                            at = (offset_of >= offset) & (offset_of < offset + count)
                            value = jnp.where(at, own, value)
                out[piece] = value


def pack_kernel(plan, early, late, halo, *outs):
    me = lax.axis_index("tx")
    lane = lane_iota()
    cols, width, parts = plan.cols, plan.width, plan.parts
    slot = lane // width

    def within(start, length):
        return ((lane - start) & (LANES - 1)) < length

    def piece_with_halo(turned, before, piece):
        number, tile = piece // plan.tiles, piece % plan.tiles
        turn = width * (piece % parts)
        value = turned[piece]
        for seg_tile, column, first, count, offset in plan.segments:
            if seg_tile != tile:
                continue
            n = (before + number) * cols + column
            remote, at = halo[n // PER_VREG], HALO * (n % PER_VREG)
            if first < HALO:
                start = (turn + offset) % LANES
                value = jnp.where(within(start, HALO - first), roll(remote, start - at - first), value)
            if first + count > width + HALO:
                begin = max(first, width + HALO)
                start = (turn + (parts - 1) * width + offset + begin - first) % LANES
                length = first + count - begin
                shift = start - at - (begin - width - HALO)
                value = jnp.where(within(start, length), roll(remote, shift), value)
        return value

    for turned, before, targets in ((early, 0, outs[:parts]), (late, len(EARLY), outs[parts:])):
        pieces = turned.shape[0]
        for group in range(-(-pieces // parts)):
            values = [
                piece_with_halo(turned, before, group * parts + j) if group * parts + j < pieces else None
                for j in range(parts)
            ]
            for m in range(parts):
                turn = (slot - (me ^ m)) & (parts - 1)
                value = values[0]
                for j in range(1, parts):
                    if values[j] is not None:
                        value = jnp.where(turn == j, values[j], value)
                targets[m][group] = value


class Geometry:
    def __init__(self, plan):
        self.plan = plan
        width, cols, parts = plan.width, plan.cols, plan.parts
        me, ty, ty_last = lax.axis_index("tx"), lax.axis_index("ty"), lax.axis_size("ty") - 1
        lane = lane_iota()
        self.offset_of = lane & (width - 1)
        slot = lane // width
        self.row_of, self.column_of = [], []
        for tile in range(plan.tiles):
            row = None
            for seg_tile, column, first, count, offset in plan.segments:
                if seg_tile == tile:
                    here_row, here_col = self.offset_of - offset + first, slot * cols + column
                    if row is None:
                        row, col = here_row, here_col
                    else:
                        inside = (self.offset_of >= offset) & (self.offset_of < offset + count)
                        row, col = jnp.where(inside, here_row, row), jnp.where(inside, here_col, col)
            self.row_of.append(row)
            self.column_of.append(col)
        block_row = me * width - HALO
        self.inner = {
            "west": [col > 0 for col in self.column_of],
            "east": [col < parts * cols - 1 for col in self.column_of],
            "south": [(row + block_row != 0) | (ty != 0) for row in self.row_of],
            "north": [(row + block_row != parts * width - 1) | (ty != ty_last) for row in self.row_of],
        }
        self.moves = {side: plan.moves(side) for side in self.inner}

    def neighbour(self, values, side):
        return shifted(values, self.moves[side], self.offset_of)

    def kept(self, side, tile, value):
        return jnp.where(self.inner[side][tile], value, 0.0)


SIDES = (
    ("west", "east", pl.ds(0, NP), -1.0),
    ("east", "west", pl.ds(NODES - NP, NP), 1.0),
    ("south", "north", pl.ds(0, NP, stride=NP), -1.0),
    ("north", "south", pl.ds(NP - 1, NP, stride=NP), 1.0),
)


def cut(value, i):
    return value[i * NP : (i + 1) * NP]


def section_adjoint(s, geometry, lift, adj_table, state, wet, speed, rub, final, later, total, gathered):
    half, drive = 0.5 * lift, PENALTY_SPEED
    neighbour, kept = geometry.neighbour, geometry.kept
    every = range(geometry.plan.tiles)
    comps = (0, 1, 2) if s < 3 else (1, 2)
    given = [WEIGHTS[s] * wet[s, t] for t in every]
    passed = [COEFS[s] * wet[s, t] if s < 3 else None for t in every]

    def masked(t, c, rows):
        value = given[t] * final[t, c - 1, rows] if c else None
        if s < 3:
            carried = passed[t] * later[s + 1, t, c, rows]
            value = carried if value is None else value + carried
        return value

    trace = {(name, c, t): masked(t, c, rows) for name, _, rows, _ in SIDES for c in comps for t in every}
    pulls, direct = {}, {}
    for name, other, _, sign in SIDES:
        for c in comps:
            beside = neighbour([trace[other, c, t] for t in every], name)
            for t in every:
                own = trace[name, c, t]
                pulls[name, c, t] = kept(name, t, (sign * half) * (own + beside[t]))
                direct[name, c, t] = kept(name, t, (half * drive) * (beside[t] - own))
    for t in every:
        cots = [[masked(t, c, pl.ds(i * NP, NP)) for i in range(NP)] for c in range(3)]
        ends = lambda c: [table[name, c, t] for table in (pulls, direct) for name in ("south", "north")]
        data = jnp.concatenate([split_data(cots[c], ends(c)) for c in comps], axis=1)
        out = jnp.dot(adj_table[...], data, preferred_element_type=F32)
        columns = {c: out[:, at * LANES : (at + 1) * LANES] for at, c in enumerate(comps)}
        for i in range(NP):
            rows = pl.ds(i * NP, NP)
            pull_x, pull_y, adds = (
                {c: cut(columns[c], k * NP + i) for c in comps} for k in range(3)
            )
            x_m, mixed, y_n = pull_x[1], pull_y[1] + pull_x[2], pull_y[2]
            to_m, to_n = adds[1], adds[2]
            if s < 3:
                to_m, to_n, to_h = to_m + pull_x[0], to_n + pull_y[0], adds[0]
            for at, name in ((0, "west"), (NP - 1, "east")):
                if i == at:
                    x_m = x_m + pulls[name, 1, t]
                    mixed = mixed + pulls[name, 2, t]
                    to_m = to_m + direct[name, 1, t]
                    to_n = to_n + direct[name, 2, t]
                    if s < 3:
                        to_m = to_m + pulls[name, 0, t]
                        to_h = to_h + direct[name, 0, t]
            h, u, v = state[s, t, 0, rows], speed[s, t, 0, rows], speed[s, t, 1, rows]
            cot_m, cot_n = cots[1][i], cots[2][i]
            drag, over = rub[s, t, 0, rows], rub[s, t, 1, rows]
            along = cot_m * u + cot_n * v
            fall = drag * along
            extra = over * along
            if gathered is not None:
                gathered[t] = gathered[t] + fall * h
            ux, vy = u * x_m, v * y_n
            first = ux + v * mixed + extra * u
            second = vy + extra * v
            later_h = h * (x_m + y_n) - u * first - v * second - (4.0 / 3.0) * fall
            if s < 3:
                later_h = later_h + to_h
            later_m = to_m + ux + first + drag * cot_m
            later_n = to_n + (vy + u * mixed) + second + drag * cot_n
            for c, value in enumerate((later_h, later_m, later_n)):
                if s == 0:
                    value = value + (later[1, t, c, rows] + later[2, t, c, rows] + later[3, t, c, rows])
                    if c:
                        value = value + final[t, c - 1, rows]
                    total[t, c, rows] = value
                else:
                    later[s, t, c, rows] = value


def roughness(man_ref, zone_row):
    zones = man_ref.shape[1]
    zone_iota = lax.broadcasted_iota(jnp.int32, (zones, LANES), 0).astype(F32)
    hot = (jnp.broadcast_to(zone_row, (zones, LANES)) == zone_iota).astype(F32)
    man = jnp.broadcast_to(man_ref[...], (8, zones))
    return hot, jnp.dot(man, hot, precision=lax.Precision.HIGHEST, preferred_element_type=F32)


def forward_kernel(plan, lift, *refs):
    parts, width, tiles = plan.parts, plan.width, plan.tiles
    messages = refs[:parts]
    man_ref, fwd_table = refs[parts : parts + 2]
    state, wet, speed, rub, final, zone, drop = refs[parts + 2 :]
    me = lax.axis_index("tx")
    half, drive = 0.5 * lift, PENALTY_SPEED
    every = range(tiles)

    for n, value in exchange_in(
        lambda m, group: messages[m][group], len(EARLY) * tiles, me, parts, width
    ):
        (array, i), tile = EARLY[n // tiles], n % tiles
        if array < 3:
            state[0, tile, array, pl.ds(i * NP, NP)] = value
        else:
            for s in range(4):
                wet[s, tile] = jnp.broadcast_to(value[s : s + 1], (8, LANES))
            zone[tile] = value
            rough = roughness(man_ref, value[4:5])[1]
            drop[tile] = -(rough * rough)
    geometry = Geometry(plan)
    neighbour, kept = geometry.neighbour, geometry.kept

    for s in range(4):
        comps = (0, 1, 2) if s < 3 else (1, 2)
        for t in every:
            for i in range(NP):
                rows = pl.ds(i * NP, NP)
                h, m, n = (state[s, t, c, rows] for c in range(3))
                inverse = 1.0 / h
                u, v = m * inverse, n * inverse
                square = u * u + v * v + SPEED_FLOOR
                over = drop[t] * (lax.rsqrt(square) * jnp.exp((-4.0 / 3.0) * jnp.log(h)))
                speed[s, t, 0, rows] = u
                speed[s, t, 1, rows] = v
                rub[s, t, 0, rows] = over * square
                rub[s, t, 1, rows] = over
        hands, keeps = {}, {}
        for name, _, rows, sign in SIDES:
            for t in every:
                h, m, n = (state[s, t, c, rows] for c in range(3))
                pressure = 0.5 * h * h
                if name in ("west", "east"):
                    u = speed[s, t, 0, rows]
                    parts_of = (m, m * u + pressure, n * u)
                else:
                    v = speed[s, t, 1, rows]
                    parts_of = (n, m * v, n * v + pressure)
                for c in comps:
                    f, q = parts_of[c], (sign * drive) * (h, m, n)[c]
                    hands[name, c, t] = f + q
                    keeps[name, c, t] = f - q
        gains = {}
        for name, other, _, sign in SIDES:
            for c in comps:
                beside = neighbour([hands[other, c, t] for t in every], name)
                for t in every:
                    gains[name, c, t] = kept(name, t, (sign * half) * (keeps[name, c, t] - beside[t]))
        for t in every:
            fluxes = [[] for _ in range(5)]
            for i in range(NP):
                rows = pl.ds(i * NP, NP)
                h, m, n = (state[s, t, c, rows] for c in range(3))
                u, v = speed[s, t, 0, rows], speed[s, t, 1, rows]
                pressure = 0.5 * h * h
                for k, value in enumerate((m, n, m * u + pressure, n * u, n * v + pressure)):
                    fluxes[k].append(value)
            columns = []
            for c in comps:
                first, second = ((0, 1), (2, 3), (3, 4))[c]
                columns.append(
                    split_data(fluxes[first] + fluxes[second], [gains["south", c, t], gains["north", c, t]])
                )
            out = jnp.dot(
                fwd_table[...], jnp.concatenate(columns, axis=1), preferred_element_type=F32
            )
            now = (COEFS[s] if s < 3 else WEIGHTS[3]) * wet[s, t]
            for at, c in enumerate(comps):
                for i in range(NP):
                    rows = pl.ds(i * NP, NP)
                    value = cut(out[:, at * LANES : (at + 1) * LANES], i)
                    if i == 0:
                        value = value + gains["west", c, t]
                    if i == NP - 1:
                        value = value + gains["east", c, t]
                    if c:
                        value = value + rub[s, t, 0, rows] * state[s, t, c, rows]
                    start = state[0, t, c, rows]
                    if s < 3:
                        state[s + 1, t, c, rows] = start + now * value
                    else:
                        middle = state[1, t, c, rows] + 2.0 * state[2, t, c, rows] + state[3, t, c, rows]
                        total = ((1.0 / 3.0) * middle - (1.0 / 3.0) * start) + now * value
                        final[t, c - 1, rows] = total


def adjoint_kernel(plan, lift, *refs):
    parts, width, tiles = plan.parts, plan.width, plan.tiles
    messages = refs[:parts]
    man_ref, adj_table, state, wet, speed, rub, reached, zone = refs[parts : parts + 8]
    rough_out, final, later = refs[parts + 8 :]
    me = lax.axis_index("tx")
    zones = man_ref.shape[1]
    every = range(tiles)
    for n, value in exchange_in(
        lambda m, group: messages[m][group], len(LATE) * tiles, me, parts, width
    ):
        i, tile = LATE[n // tiles][1], n % tiles
        rows = pl.ds(i * NP, NP)
        for c in range(2):
            final[tile, c, rows] = value * reached[tile, c, rows]
    geometry = Geometry(plan)
    row_of = geometry.row_of
    hot, rough = zip(*(roughness(man_ref, zone[t, 4:5]) for t in every))
    gathered = [jnp.zeros((8, LANES), F32) for _ in every]
    for s in (3, 2, 1):
        section_adjoint(
            s, geometry, lift, adj_table, state, wet, speed, rub, final, later, None, gathered
        )
    gather_first(state, wet, speed, rub, final, later, gathered)

    part = jnp.zeros((8, zones), F32)
    for tile in range(tiles):
        own_rows = (row_of[tile] >= HALO) & (row_of[tile] < HALO + width)
        sums = jnp.broadcast_to(jnp.sum(gathered[tile], axis=0, keepdims=True), (8, LANES))
        sums = jnp.where(own_rows, 2.0 * sums / rough[tile], 0.0)
        part = part + lax.dot_general(
            sums,
            hot[tile],
            (((1,), (1,)), ((), ())),
            precision=lax.Precision.HIGHEST,
            preferred_element_type=F32,
        )
    rough_out[...] = jnp.concatenate([part, jnp.zeros((8, LANES - zones), F32)], axis=1)


def gather_first(state, wet, speed, rub, final, later, gathered):
    for t in range(len(gathered)):
        given, passed = WEIGHTS[0] * wet[0, t], COEFS[0] * wet[0, t]
        for i in range(NP):
            rows = pl.ds(i * NP, NP)
            cot_m, cot_n = (given * final[t, c - 1, rows] + passed * later[1, t, c, rows] for c in (1, 2))
            along = cot_m * speed[0, t, 0, rows] + cot_n * speed[0, t, 1, rows]
            gathered[t] = gathered[t] + rub[0, t, 0, rows] * along * state[0, t, 0, rows]


def answer_kernel(plan, lift, adj_table, state, wet, speed, rub, final, later, *refs):
    parts, width, cols = plan.parts, plan.width, plan.cols
    outs, total = refs[:parts], refs[parts]
    me = lax.axis_index("tx")
    geometry = Geometry(plan)
    offset_of = geometry.offset_of
    section_adjoint(0, geometry, lift, adj_table, state, wet, speed, rub, final, later, total, None)

    def own_piece(c, i, column):
        value = None
        for tile, seg_col, first, count, offset in plan.segments:
            begin, end = max(first, HALO), min(first + count, HALO + width)
            if seg_col != column or begin >= end:
                continue
            moved = roll(total[tile, c, pl.ds(i * NP, NP)], (begin - HALO) - (offset + begin - first))
            if value is None:
                value = moved
            else:
                value = jnp.where((offset_of >= begin - HALO) & (offset_of < end - HALO), moved, value)
        return value

    pieces = [
        functools.partial(own_piece, c, i, column) for c in range(3) for i in range(NP) for column in range(cols)
    ]

    def put(m, group, value):
        outs[m][group] = value

    exchange_out(pieces, put, me, parts, width)


def stamp_kernel(parts, *refs):
    mine, other, outs = refs[parts], refs[parts + 1], refs[parts + 2 :]
    total = mine[...] + other[...]
    for out in outs:
        out[out.shape[0] - 1] = total


def finish_kernel(plan, *refs):
    parts, width, cols = plan.parts, plan.width, plan.cols
    messages = refs[:parts]
    (out,) = refs[parts:]
    me = lax.axis_index("tx")
    count = 3 * NP * cols
    for n, value in exchange_in(lambda m, group: messages[m][group], count, me, parts, width):
        plane, column = n // cols, n % cols
        out[plane, pl.ds(column, NP, stride=cols), :] = value


def call(kernel, outs, scratch=(), flops=1000000):
    return pl.pallas_call(
        kernel,
        out_shape=outs,
        scratch_shapes=scratch,
        compiler_params=pltpu.CompilerParams(vmem_limit_bytes=16 << 20),
        cost_estimate=pl.CostEstimate(flops=flops, bytes_accessed=1000000, transcendentals=0),
    )


def xor_swap(value, axis, bits):
    count = lax.axis_size(axis)
    return lax.ppermute(value, axis, [(i, i ^ bits) for i in range(count)])


def sum_over(value, axis):
    count, bit = lax.axis_size(axis), 1
    while bit < count:
        if 4 * bit <= count:
            one, two, three = (xor_swap(value, axis, k * bit) for k in (1, 2, 3))
            value = (value + one) + (two + three)
            bit *= 4
        else:
            value = value + xor_swap(value, axis, bit)
            bit *= 2
    return value


def local(depth0, momentum0, obs_weight, wet_mask, zone_id, manning):
    table, lift = node_tables()
    cols, rows = depth0.shape[3], depth0.shape[4]
    parts = lax.axis_size("tx")
    plan = Plan(parts, cols, rows)
    zones = manning.shape[0]
    depth = depth0.reshape(NP, NP * cols, rows)
    momentum = momentum0.reshape(2 * NP, NP * cols, rows)
    weight = obs_weight.reshape(NP, NP * cols, rows)
    fields = (depth, momentum, weight, wet_mask, zone_id)

    def out(*shape):
        return jax.ShapeDtypeStruct(shape, F32)

    along_i, along_j = np.kron(table, np.eye(NP)), np.kron(np.eye(NP), table)
    ends = np.concatenate([np.kron(np.eye(NP), np.eye(NP)[:, k : k + 1]) for k in (0, NP - 1)], axis=1)
    none = np.zeros_like(ends)
    fwd_table = split_table(np.concatenate([-along_i, -along_j], axis=1), ends)
    adj_table = split_table(
        np.concatenate([-along_i.T, -along_j.T, np.zeros_like(along_i)], axis=0),
        np.block([[none, none], [ends, none], [none, ends]]),
    )
    groups = -(-len(SOURCES) * cols // PER_VREG)
    inputs = fields + (manning.reshape(1, zones), jnp.asarray(fwd_table), jnp.asarray(adj_table))
    inputs = tuple(pltpu.with_memory_space_constraint(x, pltpu.HBM) for x in inputs)
    results = pl.pallas_call(
        functools.partial(halo_kernel, cols),
        out_shape=[jax.ShapeDtypeStruct(x.shape, x.dtype) for x in inputs] + [out(groups, 8, LANES)],
        in_specs=[pl.BlockSpec(memory_space=pltpu.HBM)] * len(inputs),
        scratch_shapes=[pltpu.SemaphoreType.DMA((sum(len(chunks(x.shape[0])) for x in inputs),))],
        compiler_params=pltpu.CompilerParams(vmem_limit_bytes=16 << 20),
        cost_estimate=pl.CostEstimate(flops=1000000, bytes_accessed=1000000, transcendentals=0),
    )(*inputs)
    fields, man, tables, halo = results[:5], results[5], results[6:8], results[8]
    if lax.axis_size("ty") > 1:
        assert lax.axis_size("ty") == 2
        halo = xor_swap(halo, "ty", 1)
    pieces = [len(sources) * plan.tiles for sources in (EARLY, LATE)]
    counts = [-(-count // parts) for count in pieces]
    turned = call(functools.partial(turn_kernel, plan), [out(count, 8, LANES) for count in pieces])(*fields)
    sent = call(
        functools.partial(pack_kernel, plan), [out(count, 8, LANES) for count in counts for _ in range(parts)]
    )(*turned, halo)
    received = [sent[0]] + [xor_swap(sent[m], "tx", m) for m in range(1, parts)]
    weights = [sent[parts]] + [xor_swap(sent[parts + m], "tx", m) for m in range(1, parts)]

    back = -(-3 * NP * cols // parts)
    t = plan.tiles
    shapes = [
        (4, t, 3, NODES, LANES),
        (4, t, NP, LANES),
        (4, t, 2, NODES, LANES),
        (4, t, 2, NODES, LANES),
        (t, 2, NODES, LANES),
        (4, t, 3, NODES, LANES),
    ]
    *kept, zone = call(
        functools.partial(forward_kernel, plan, lift),
        [out(*shape) for shape in shapes[:5]] + [out(t, NP, LANES)],
        [pltpu.VMEM((t, NP, LANES), F32)],
    )(*received, man, tables[0])
    rough, final, later = call(
        functools.partial(adjoint_kernel, plan, lift), [out(8, LANES)] + [out(*shape) for shape in shapes[4:]]
    )(*weights, man, tables[1], *kept, zone)
    kept = kept[:4] + [final, later]
    answers = call(
        functools.partial(answer_kernel, plan, lift),
        [out(back + 1, 8, LANES)] * parts,
        [pltpu.VMEM((t, 3, NODES, LANES), F32)],
    )(tables[1], *kept)
    other = jnp.zeros_like(rough)
    if lax.axis_size("ev") == 2:
        other = xor_swap(rough, "ev", 1)
    elif lax.axis_size("ev") > 1:
        rough = sum_over(rough, "ev")
    space = pl.BlockSpec(memory_space=pltpu.VMEM)
    answers = pl.pallas_call(
        functools.partial(stamp_kernel, parts),
        out_shape=[out(back + 1, 8, LANES)] * parts,
        in_specs=[pl.BlockSpec(memory_space=pl.ANY)] * parts + [space] * 2,
        out_specs=[space] * parts,
        input_output_aliases={m: m for m in range(parts)},
        compiler_params=pltpu.CompilerParams(vmem_limit_bytes=16 << 20),
        cost_estimate=pl.CostEstimate(flops=1000, bytes_accessed=1000, transcendentals=0),
    )(*answers, rough, other)
    answers = [answers[0]] + [xor_swap(answers[m], "tx", m) for m in range(1, parts)]
    sums = [answer[back] for answer in answers]
    while len(sums) > 1:
        sums = [one + two for one, two in zip(sums[::2], sums[1::2])]
    rough = sum_over(sums[0], "ty")
    adjoint = call(functools.partial(finish_kernel, plan), out(3 * NP, NP * cols, rows))(*answers)
    events_all = depth0.shape[0] * lax.axis_size("ev")
    scale = zones / (TIME_STEP * events_all * cols * parts * rows * lax.axis_size("ty") * NODES)
    return (adjoint.reshape(1, 3, NP, NP, cols, rows), rough[0, :zones] * scale)


def solution(mesh):
    in_specs = (
        P(("basin", "ev"), None, None, "tx", "ty"),
        P(("basin", "ev"), None, None, None, "tx", "ty"),
        P(("basin", "ev"), None, None, "tx", "ty"),
        P(("basin", "ev"), None, "tx", "ty"),
        P(("basin", "tx"), "ty"),
        P("basin"),
    )
    out_specs = (P(("basin", "ev"), None, None, None, "tx", "ty"), P("basin"))
    return jax.shard_map(local, mesh=mesh, in_specs=in_specs, out_specs=out_specs, check_vma=False)
```
